512 devices in a mesh: seq: 4 (over y_lo, core), blk: 128 (over z, y_hi, x).
Axes of the slice: x: 4, y: 4 (y_hi: 2, y_lo: 2; y = y_hi * 2 + y_lo), z: 16, core: 2. Of those that a mesh axis runs over, the one named last changes fastest.
Arguments:
- tokens: bfloat16 [65536, 1024], P(('seq', 'blk')), may hold values from -6 to 6
- cotangent: bfloat16 [65536, 1024], P(('seq', 'blk')), may hold values from -6 to 6
- routes: int32 [65536, 2], P(('seq', 'blk')), may hold values from 0 to 63, all different within a row; in each aligned block of 128 rows (0 to 127, 128 to 255, ...) at most 8 rows name the same one
- gate_codes: int32 [65536, 2], P(('seq', 'blk')), may hold values from 1 to 64
- dropout_key: int32 [2], replicated, may hold values from 0 to 1073741823
- w_gate: bfloat16 [128, 1024, 352], P('blk', 'seq'), may hold values from -0.1875 to 0.1875
- w_up: bfloat16 [128, 1024, 352], P('blk', 'seq'), may hold values from -0.1875 to 0.1875
- w_down: bfloat16 [128, 352, 1024], P('blk', None, 'seq'), may hold values from -0.21875 to 0.21875
Outputs:
- layer_out: bfloat16 [65536, 1024], P(('seq', 'blk'))
- tokens_grad: bfloat16 [65536, 1024], P(('seq', 'blk'))
- gate_grad: bfloat16 [128, 1024, 352], P('blk', 'seq')
- up_grad: bfloat16 [128, 1024, 352], P('blk', 'seq')
- down_grad: bfloat16 [128, 352, 1024], P('blk', None, 'seq')
The draws below stay inside these ranges and needn't reach their ends.
Inputs may be any that keep to these rules, and one draw needn't show every extreme that they name: `routes`: each row names 2 different experts; in the 128 rows of one device no expert is named more than 8 times.
All inputs are finite; a program needn't handle non-finite values.
Results may differ from the reference program's by a relative error of at most 0.0095.
Values may be sent and summed in bfloat16 or wider, within the bound.
A program may use at most 64 MiB of HBM per device.

```python
import math
import jax
import jax.numpy as jnp
import numpy as np
from jax import lax

D = 1024
FF = 704
TOP = 2
TOK_DEV = 128
EXPERTS = 64
CAP = 8
TOK_GROUP = 16384
TOKENS = 65536
N_SEQ = 4
N_BLK = 128


def touch_ends(entries, stream_key, smallest, top_value):
    extent = entries.shape
    index_at = [jax.random.randint(jax.random.fold_in(stream_key, axis), (), 0, extent[axis]) for axis in range(len(extent))]
    entries = entries.at[tuple(index_at)].set(smallest)
    longest = extent.index(max(extent))
    index_at[longest] = (index_at[longest] + 1) % extent[longest]
    return entries.at[tuple(index_at)].set(top_value)


def level_of(stream_key, dims, split, low, largest):
    level = 1.0
    for axis_at, blocks in split:
        steps = jax.random.uniform(jax.random.fold_in(jax.random.fold_in(stream_key, 6), axis_at), (blocks,), jnp.float32, low / len(split), largest / len(split))
        level = level * jnp.repeat(jnp.exp(steps), dims[axis_at] // blocks).reshape((-1,) + (1,) * (len(dims) - 1 - axis_at))
    return level


def routed_block(key, own, number, rows, number_of, top, bound, lean):
    ranking = jax.random.permutation(key, number_of)
    packed, usual = shares(number_of, rows * top, bound, lean, True), shares(number_of, rows * top, bound, lean, False)
    places = jnp.arange(number_of)

    def named(lengths, offset_by):
        used = int((lengths > 0).sum())
        fixed = max(1, used // 4)
        passed = fixed + (places - fixed + offset_by * (used - fixed)) % max(1, number_of - fixed)
        return jnp.zeros((number_of,), jnp.int32).at[ranking[jnp.where(places < fixed, places, passed)]].set(jnp.asarray(lengths, jnp.int32))

    lengths = jnp.where(number % 4 == 0, named(packed, number // 4), named(usual, number - number // 4 - 1))
    mixed = jax.random.permutation(jax.random.fold_in(own, 3), number_of)
    donor, sink = mixed[0:number_of // 2 * 2:2], mixed[1:number_of // 2 * 2:2]
    room = jnp.minimum(lengths[donor] - 1, bound - lengths[sink]) // 2
    room = jnp.where((donor == ranking[0]) | (sink == ranking[0]) | (lengths[sink] == 0), 0, jnp.maximum(room, 0))
    passed = jax.random.randint(jax.random.fold_in(own, 4), (number_of // 2,), 0, 1 << 20) % (room + 1)
    lengths = lengths.at[donor].add(-passed).at[sink].add(passed)
    labels = jnp.searchsorted(jnp.cumsum(lengths), jnp.arange(rows * top), side="right").astype(jnp.int32)
    listing = labels.reshape(top, rows).T
    listing = listing[jax.random.permutation(jax.random.fold_in(own, 1), rows)]
    offset_by = jax.random.randint(jax.random.fold_in(own, 2), (rows, 1), 0, top)
    return jnp.take_along_axis(listing, (jnp.arange(top)[None, :] + offset_by) % top, axis=1)


def shares(amount, total, most, skew, full):
    weights = [(1 << 20) // math.isqrt(grade ** skew) + 1 for grade in range(1, amount + 1)]
    largest = most if full else min(most, max(-(-total // amount), total * weights[0] // sum(weights)))
    least = 1 if total - largest >= amount - 1 else 0
    given, surplus = [largest] + [least] * (amount - 1), total - largest - least * (amount - 1)
    while surplus > 0:
        candidates = [i for i in range(1, amount) if given[i] < largest] or [i for i in range(1, amount) if given[i] < most]
        whole, remaining = sum([weights[i] for i in candidates]), surplus
        for i in candidates:
            extra = min(most - given[i], max(1, remaining * weights[i] // whole), surplus)
            given[i] = given[i] + extra
            surplus = surplus - extra
    return np.array(given)


def bell_draw(key, dims, spread, most, cuts=(), kind=jnp.bfloat16):
    loudness = level_of(key, dims, cuts, -0.22, 0.18) if cuts else 1.0
    result = jax.random.normal(key, dims, jnp.float32) * spread * loudness
    return jnp.minimum(jnp.maximum(result, -most), most).astype(kind)


def setup_inputs(seed: int = 0) -> dict:
    splits = jax.random.split(jax.random.key(seed), 9)
    tokens = bell_draw(splits[0], (TOKENS, D), 1.0, 6.0, ((0, 512),))
    cotangent = bell_draw(splits[1], (TOKENS, D), 1.0, 6.0, ((0, 512),))
    routes_keys = jax.random.split(jax.random.fold_in(splits[2], 1), TOKENS // TOK_DEV)
    routes_turns = jax.random.permutation(jax.random.fold_in(splits[2], 3), TOKENS // TOK_DEV)
    routes = jax.vmap(lambda own, number: routed_block(jax.random.fold_in(splits[2], 2), own, number, TOK_DEV, EXPERTS, TOP, CAP, 2))(routes_keys, routes_turns).reshape((TOKENS, TOP))
    gate_codes = touch_ends(jax.random.randint(splits[3], (TOKENS, TOP), 1, 65), jax.random.fold_in(splits[3], 1), 1, 64).astype(jnp.int32)
    dropout_key = jax.random.randint(splits[4], (2,), 0, 1073741824).astype(jnp.int32)
    w_gate = bell_draw(splits[5], (2 * EXPERTS, D, FF // 2), D ** -0.5, 0.1875, ((0, 128), (1, 4)))
    w_up = bell_draw(splits[6], (2 * EXPERTS, D, FF // 2), D ** -0.5, 0.1875, ((0, 128), (1, 4)))
    w_down = bell_draw(splits[7], (2 * EXPERTS, FF // 2, D), FF ** -0.5, 0.21875, ((0, 128), (2, 4)))
    return {"tokens": tokens, "cotangent": cotangent, "routes": routes, "gate_codes": gate_codes, "dropout_key": dropout_key, "w_gate": w_gate, "w_up": w_up, "w_down": w_down}


mixing_factor = 73244475


def scramble(values):
    values = values ^ ((values >> 16) & 65535)
    values = values * mixing_factor
    values = values ^ ((values >> 16) & 65535)
    values = values * mixing_factor
    return values ^ ((values >> 16) & 65535)


def keep_scale(token_ids, columns, key_pair):
    base_hash = scramble(key_pair[0] ^ scramble(key_pair[1]))
    mixed_ids = scramble(token_ids ^ base_hash)
    hashed = scramble(mixed_ids[:, None] ^ (columns[None, :] * 40503))
    return jnp.where((hashed & 1023) >= 128, jnp.float32(8.0 / 7.0), jnp.float32(0.0))


def reference(tokens, cotangent, routes, gate_codes, dropout_key, w_gate, w_up, w_down):
    expert_count = w_gate.shape[0] // 2
    half_width = w_gate.shape[2]
    hidden_width = 2 * half_width
    model_width = w_gate.shape[1]
    gate_full = w_gate.reshape(expert_count, 2, model_width, half_width).transpose(0, 2, 1, 3).reshape(expert_count, model_width, hidden_width)
    up_full = w_up.reshape(expert_count, 2, model_width, half_width).transpose(0, 2, 1, 3).reshape(expert_count, model_width, hidden_width)
    down_full = w_down.reshape(expert_count, hidden_width, model_width)
    pair_count = TOKENS * TOP
    pair_expert = routes.reshape(-1).astype(jnp.int32)
    pair_token = (jnp.arange(pair_count) // TOP).astype(jnp.int32)
    pair_gate = gate_codes.reshape(-1).astype(jnp.float32) / 64.0
    pair_group = pair_token // TOK_GROUP
    segment_key = pair_expert * N_SEQ + pair_group
    sorted_order = jnp.argsort(segment_key, stable=True).astype(jnp.int32)
    segment_total = expert_count * N_SEQ
    seg_counts = jax.ops.segment_sum(jnp.ones(pair_count, jnp.int32), segment_key, num_segments=segment_total)
    seg_starts = jnp.cumsum(seg_counts) - seg_counts
    seg_length = N_BLK * CAP
    positions = jnp.arange(seg_length, dtype=jnp.int32)
    valid_slot = positions[None, :] < seg_counts[:, None]
    clipped = jnp.clip(seg_starts[:, None] + positions[None, :], 0, pair_count - 1).astype(jnp.int32)
    slot_pairs = jnp.where(valid_slot, sorted_order[clipped], 0)
    key_pair = dropout_key.astype(jnp.int32)

    def per_expert(carried, expert):
        out_acc, grad_acc = carried
        gate_mat = gate_full[expert]
        up_mat = up_full[expert]
        down_mat = down_full[expert]
        columns = expert * hidden_width + jnp.arange(hidden_width, dtype=jnp.int32)
        sums_gate = jnp.zeros((model_width, hidden_width), jnp.float32)
        sums_up = jnp.zeros((model_width, hidden_width), jnp.float32)
        sums_down = jnp.zeros((hidden_width, model_width), jnp.float32)
        for group_index in range(N_SEQ):
            chosen = slot_pairs[expert * N_SEQ + group_index]
            live_slot = valid_slot[expert * N_SEQ + group_index]
            token_of = pair_token[chosen]
            weight_of = jnp.where(live_slot, pair_gate[chosen], 0.0)
            inputs = tokens[token_of] * live_slot[:, None].astype(tokens.dtype)
            drop_scale = keep_scale(token_of, columns, key_pair)
            gate_pre = jnp.dot(inputs, gate_mat, preferred_element_type=jnp.float32)
            up_pre = jnp.dot(inputs, up_mat, preferred_element_type=jnp.float32)
            sigmoid_gate = jax.nn.sigmoid(gate_pre)
            silu_gate = gate_pre * sigmoid_gate
            hidden = (silu_gate * up_pre * drop_scale).astype(jnp.bfloat16)
            expert_out = jnp.dot(hidden, down_mat, preferred_element_type=jnp.float32)
            slot_cot = (weight_of[:, None] * cotangent[token_of].astype(jnp.float32)).astype(jnp.bfloat16)
            hidden_grad = jnp.dot(slot_cot, down_mat.T, preferred_element_type=jnp.float32) * drop_scale
            gate_pre_grad = (hidden_grad * up_pre * sigmoid_gate * (1.0 + gate_pre * (1.0 - sigmoid_gate))).astype(jnp.bfloat16)
            up_pre_grad = (hidden_grad * silu_gate).astype(jnp.bfloat16)
            input_grad = jnp.dot(gate_pre_grad, gate_mat.T, preferred_element_type=jnp.float32) + jnp.dot(up_pre_grad, up_mat.T, preferred_element_type=jnp.float32)
            out_acc = out_acc.at[token_of].add(weight_of[:, None] * expert_out)
            grad_acc = grad_acc.at[token_of].add(jnp.where(live_slot[:, None], input_grad, 0.0))
            piece_gate = jnp.dot(inputs.T, gate_pre_grad, preferred_element_type=jnp.float32)
            piece_up = jnp.dot(inputs.T, up_pre_grad, preferred_element_type=jnp.float32)
            piece_down = jnp.dot(hidden.T, slot_cot, preferred_element_type=jnp.float32)
            sums_gate = sums_gate + lax.optimization_barrier(piece_gate.astype(jnp.bfloat16)).astype(jnp.float32)
            sums_up = sums_up + lax.optimization_barrier(piece_up.astype(jnp.bfloat16)).astype(jnp.float32)
            sums_down = sums_down + lax.optimization_barrier(piece_down.astype(jnp.bfloat16)).astype(jnp.float32)
        return (out_acc, grad_acc), (sums_gate.astype(jnp.bfloat16), sums_up.astype(jnp.bfloat16), sums_down.astype(jnp.bfloat16))

    start_acc = (jnp.zeros((TOKENS, model_width), jnp.float32), jnp.zeros((TOKENS, model_width), jnp.float32))
    finals, stacked = lax.scan(per_expert, start_acc, jnp.arange(expert_count, dtype=jnp.int32))
    gate_grad = stacked[0].reshape(expert_count, model_width, 2, half_width).transpose(0, 2, 1, 3).reshape(2 * expert_count, model_width, half_width)
    up_grad = stacked[1].reshape(expert_count, model_width, 2, half_width).transpose(0, 2, 1, 3).reshape(2 * expert_count, model_width, half_width)
    down_grad = stacked[2].reshape(2 * expert_count, half_width, model_width)
    return (finals[0].astype(jnp.bfloat16), finals[1].astype(jnp.bfloat16), gate_grad, up_grad, down_grad)
```

```python
import jax
import jax.numpy as jnp
from jax import lax
from jax.sharding import PartitionSpec as P

mixing_factor = 73244475
contract_last = (((1,), (1,)), ((), ()))
contract_first = (((0,), (0,)), ((), ()))


def scramble(values):
    values = values ^ values >> 16 & 65535
    values = values * mixing_factor
    values = values ^ values >> 16 & 65535
    values = values * mixing_factor
    return values ^ values >> 16 & 65535


def keep_scale(token_ids, columns, key_pair):
    base_hash = scramble(key_pair[0] ^ scramble(key_pair[1]))
    mixed_ids = scramble(token_ids ^ base_hash)
    hashed = scramble(mixed_ids[:, None] ^ columns[None, :] * 40503)
    return jnp.where(hashed & 1023 >= 128, jnp.float32(8.0 / 7.0), jnp.float32(0.0))


def mm(a, b, dims=(((1,), (0,)), ((), ()))):
    return lax.dot_general(a, b, dims, preferred_element_type=jnp.float32)


def local(tokens, cotangent, routes, gate_codes, dropout_key, w_gate, w_up, w_down):
    block_count = lax.axis_size("blk")
    seq_index = lax.axis_index("seq")
    blk_index = lax.axis_index("blk")
    tok_rows, model_width = tokens.shape
    top_count = routes.shape[1]
    expert_count = block_count // 2
    capacity = 2 * tok_rows * top_count // expert_count
    part = capacity // 2
    half = w_gate.shape[2]
    parity = blk_index % 2
    expert_here = blk_index // 2
    bf = jnp.bfloat16

    pair_expert = routes.reshape(-1)
    one_hot = (pair_expert[:, None] == jnp.arange(expert_count, dtype=jnp.int32)[None, :]).astype(bf)
    pairs = tok_rows * top_count
    lower = (jnp.arange(pairs)[:, None] > jnp.arange(pairs)[None, :]).astype(bf)
    before = mm(lower, one_hot)
    position = jnp.sum(before * one_hot.astype(jnp.float32), axis=1).astype(jnp.int32)
    slot_index = (pair_expert * capacity + position).reshape(tok_rows, top_count)
    slot_total = expert_count * capacity
    slots = jnp.arange(slot_total, dtype=jnp.int32)
    gates = gate_codes.astype(jnp.float32) / 64.0
    hit = slots[:, None, None] == slot_index[None]
    select = jnp.sum(hit, axis=2).astype(bf)
    weigh = jnp.sum(jnp.where(hit, gates[None], 0.0), axis=2).astype(bf)
    local_ids = jnp.sum(jnp.where(hit, jnp.arange(tok_rows, dtype=jnp.int32)[None, :, None], 0), axis=(1, 2))

    send = jnp.concatenate([mm(select, tokens).astype(bf), mm(weigh, cotangent).astype(bf)], axis=1)
    send = send.reshape(block_count, part, 2 * model_width)
    recv_ids = lax.all_to_all(local_ids.reshape(block_count, part), "blk", 0, 0, tiled=True)
    recv = lax.all_to_all(send, "blk", split_axis=0, concat_axis=0, tiled=True)

    swap = [(i, i ^ 1) for i in range(block_count)]
    first = parity == 0

    def both(own):
        other = lax.ppermute(own, "blk", swap)
        return jnp.where(first, own, other), jnp.where(first, other, own)

    g0, g1 = both(w_gate[0])
    u0, u1 = both(w_up[0])
    d0, d1 = both(w_down[0])
    gate_mat = lax.all_gather(jnp.concatenate([g0, g1], axis=1), "seq", axis=0, tiled=True)
    up_mat = lax.all_gather(jnp.concatenate([u0, u1], axis=1), "seq", axis=0, tiled=True)
    down_mat = lax.all_gather(jnp.concatenate([d0, d1], axis=0), "seq", axis=1, tiled=True)

    rows = block_count * part
    row_ids = (
        (seq_index * block_count + jnp.arange(block_count, dtype=jnp.int32)) * tok_rows
    )[:, None] + recv_ids
    row_ids = row_ids.reshape(rows)
    columns = expert_here * (2 * half) + jnp.arange(2 * half, dtype=jnp.int32)
    recv = recv.reshape(rows, 2 * model_width)
    inputs = recv[:, :model_width]
    cot = recv[:, model_width:]

    drop = keep_scale(row_ids, columns, dropout_key)
    gate_pre = mm(inputs, gate_mat)
    up_pre = mm(inputs, up_mat)
    sig = jax.nn.sigmoid(gate_pre)
    silu = gate_pre * sig
    hidden = (silu * up_pre * drop).astype(bf)
    expert_out = mm(hidden, down_mat).astype(bf)
    hidden_grad = mm(cot, down_mat, contract_last) * drop
    gate_pre_grad = (hidden_grad * up_pre * sig * (1.0 + gate_pre * (1.0 - sig))).astype(bf)
    up_pre_grad = (hidden_grad * silu).astype(bf)
    input_grad = (mm(gate_pre_grad, gate_mat, contract_last) + mm(up_pre_grad, up_mat, contract_last)).astype(bf)

    back = jnp.concatenate([expert_out, input_grad], axis=1).reshape(block_count, part, 2 * model_width)
    returned = lax.all_to_all(back, "blk", split_axis=0, concat_axis=0, tiled=True)

    part_gate = mm(inputs, gate_pre_grad, contract_first)
    part_up = mm(inputs, up_pre_grad, contract_first)
    part_down = mm(hidden, cot, contract_first)

    def paired(low, high):
        theirs = jnp.where(first, high, low).astype(bf)
        ours = jnp.where(first, low, high)
        return (ours + lax.ppermute(theirs, "blk", swap).astype(jnp.float32)).astype(bf)

    gate_grad = lax.psum_scatter(paired(part_gate[:, :half], part_gate[:, half:]), "seq", scatter_dimension=0, tiled=True)
    up_grad = lax.psum_scatter(paired(part_up[:, :half], part_up[:, half:]), "seq", scatter_dimension=0, tiled=True)
    down_grad = lax.psum_scatter(paired(part_down[:half], part_down[half:]), "seq", scatter_dimension=1, tiled=True)

    returned = returned.reshape(slot_total, 2 * model_width)
    layer_out = mm(weigh, returned[:, :model_width], contract_first).astype(bf)
    tokens_grad = mm(select, returned[:, model_width:], contract_first).astype(bf)
    return (layer_out, tokens_grad, gate_grad[None], up_grad[None], down_grad[None])


def solution(mesh):
    rows = P(("seq", "blk"), None)
    wide = P("blk", "seq", None)
    down = P("blk", None, "seq")
    return jax.shard_map(
        local,
        mesh=mesh,
        in_specs=(rows, rows, rows, rows, P(), wide, wide, down),
        out_specs=(rows, rows, wide, wide, down),
        check_vma=False,
    )
```
